32 devices in a mesh: band: 8 (over y, x, core), strip: 4 (over z).
Axes of the slice: x: 2, y: 2, z: 4, core: 2. Of those that a mesh axis runs over, the one named last changes fastest.
Arguments:
- pattern: int32 [16384, 2048], P(('band', 'strip')), may hold values from 0 to 2, as said below
Outputs:
- dose: float32 [16384, 2048], P(('band', 'strip'))
- exposure: float32 [16384, 2048], P(('band', 'strip'))
The draws below stay inside these ranges and needn't reach their ends.
Inputs may be any that keep to these rules, and one draw needn't show every extreme that they name: `pattern`: class codes: 0 clear, 1 feature interior, 2 feature edge.
All inputs are finite; a program needn't handle non-finite values.
Results may differ from the reference program's by a relative error of at most 0.0003.
Values sent between devices are 32-bit elements; how exact they have to be, the bound alone decides.
A program may use at most 64 MiB of HBM per device.

```python
import math
import jax
import jax.numpy as jnp
from jax import lax

W = 2048
R = 512
POOL = 256
H = 16
ITERS = 2
NR = 16384
NRC = 64
NCC = 8


def draw_pattern(key, part):
    tile = max(1, POOL // 8)
    key_level, key_roll, key_kind, key_cap = jax.random.split(jax.random.fold_in(key, 11), 4)
    order = jax.random.permutation(key_cap, 8)
    caps = jnp.where(order < 4, 1, 5).astype(jnp.int32)
    tile_rows = NR // tile
    segment = (jnp.arange(tile_rows).astype(jnp.int32) * tile * 8 // NR).astype(jnp.int32)
    row_cap = caps[segment][:, None]
    raw = jax.random.randint(key_level, (tile_rows, W // tile), 0, 60)
    level = (raw % (row_cap + 1)).astype(jnp.int32)
    level = jnp.repeat(jnp.repeat(level, tile, axis=0), tile, axis=1)
    roll = jax.random.randint(key_roll, (NR, W), 0, 4)
    kind = jax.random.randint(key_kind, (NR, W), 1, 3)
    return jnp.where(roll < level, kind, 0).astype(jnp.int32)


def setup_inputs(seed: int = 0) -> dict:
    seeds = jax.random.split(jax.random.key(seed), 2)
    pattern = draw_pattern(jax.random.fold_in(seeds[1], 71), 0)
    return dict(pattern=pattern)


ETA_BACK = 0.75
SIGMA_BACK = 6.0

def fine_weight(diff):
    spread = H / 3.0
    steps = jnp.arange(-H, H + 1).astype(jnp.float32)
    total = jnp.sum(jnp.exp(-steps * steps / (2.0 * spread * spread)))
    inside = jnp.abs(diff) <= H
    return jnp.where(inside, jnp.exp(-diff * diff / (2.0 * spread * spread)) / total, 0.0).astype(jnp.float32)

def back_weight(diff, fog_sigma):
    near = jnp.exp(-diff * diff / (2.0 * SIGMA_BACK * SIGMA_BACK)) / (SIGMA_BACK * math.sqrt(2.0 * math.pi))
    far = jnp.exp(-diff * diff / (2.0 * fog_sigma * fog_sigma)) / (fog_sigma * math.sqrt(2.0 * math.pi))
    return (0.5 * near + 0.5 * far).astype(jnp.float32)

def reference(pattern):
    dose = jnp.where(pattern == 1, 1.0, jnp.where(pattern == 2, 1.4, 0.0)).astype(jnp.float32)
    taps = fine_weight(jnp.arange(-H, H + 1).astype(jnp.float32))
    fog_sigma = NRC / 4.0
    coarse_idx = jnp.arange(NRC).astype(jnp.float32)
    kernel_rows = back_weight(coarse_idx[None, :] - coarse_idx[:, None], fog_sigma)
    col_idx = jnp.arange(NCC).astype(jnp.float32)
    kernel_cols = back_weight(col_idx[:, None] - col_idx[None, :], fog_sigma)
    block_count = NR // R

    def iterate(step, carry):
        dose_now, previous = carry
        coarse = dose_now.reshape(NRC, POOL, NCC, POOL).sum(axis=(1, 3)) / (POOL * POOL)
        back = jnp.dot(kernel_rows, coarse, precision=lax.Precision.HIGHEST, preferred_element_type=jnp.float32)
        back = jnp.dot(back, kernel_cols, precision=lax.Precision.HIGHEST, preferred_element_type=jnp.float32)
        back_rows = jnp.repeat(back, POOL, axis=0)
        padded = jnp.pad(dose_now, ((H, H), (0, 0)))

        def one_block(index):
            start = (index * R).astype(jnp.int32)
            window = lax.dynamic_slice_in_dim(padded, start, R + 2 * H, 0)
            rows_blur = jnp.zeros((R, W), window.dtype)
            for shift in range(2 * H + 1):
                rows_blur = rows_blur + taps[shift] * window[shift:shift + R]
            padded_cols = jnp.pad(rows_blur, ((0, 0), (H, H)))
            forward = jnp.zeros_like(rows_blur)
            for shift in range(2 * H + 1):
                forward = forward + taps[shift] * padded_cols[:, shift:shift + W]
            local_back = lax.dynamic_slice_in_dim(back_rows, start, R, 0)
            upsampled = jnp.repeat(local_back, POOL, axis=1)
            exposure = (forward + ETA_BACK * upsampled) / (1.0 + ETA_BACK)
            local_pattern = lax.dynamic_slice_in_dim(pattern, start, R, 0)
            occupancy = (local_pattern > 0).astype(jnp.float32)
            target = jnp.where(local_pattern == 1, 0.5, jnp.where(local_pattern == 2, 0.55, 0.0)).astype(jnp.float32)
            local_dose = lax.dynamic_slice_in_dim(dose_now, start, R, 0)
            new_dose = occupancy * (local_dose + target - exposure)
            return (new_dose, exposure)
        new_blocks, exposure_blocks = lax.map(one_block, jnp.arange(block_count).astype(jnp.int32))
        return (new_blocks.reshape(NR, W), exposure_blocks.reshape(NR, W))
    dose, exposure = lax.fori_loop(0, ITERS, iterate, (dose, jnp.zeros_like(dose)))
    return (dose, exposure)
```

```python
import functools
import math

import jax
import jax.numpy as jnp
import numpy as np
from jax import lax
from jax.experimental import pallas as pl
from jax.experimental.pallas import tpu as pltpu
from jax.sharding import PartitionSpec as P

POOL = 256
H = 16
ETA_BACK = 0.75
SIGMA_BACK = 6.0
TILE = 160
LANES = 128
MESH = pl.DeviceIdType.MESH


def fine_taps():
    spread = H / 3.0
    steps = np.arange(-H, H + 1).astype(np.float64)
    taps = np.exp(-steps * steps / (2.0 * spread * spread))
    return taps / taps.sum()


def band(rows, cols, offset):
    taps = fine_taps()
    out = np.zeros((rows, cols))
    for r in range(rows):
        for k in range(2 * H + 1):
            c = r + k + offset
            if 0 <= c < cols:
                out[r, c] = taps[k]
    return out


def split(value):
    high = value.astype(jnp.bfloat16)
    low = (value - high.astype(np.float64)).astype(jnp.bfloat16)
    return high, low


def back_np(diff, fog_sigma):
    near = np.exp(-diff * diff / (2.0 * SIGMA_BACK * SIGMA_BACK)) / (SIGMA_BACK * math.sqrt(2.0 * math.pi))
    far = np.exp(-diff * diff / (2.0 * fog_sigma * fog_sigma)) / (fog_sigma * math.sqrt(2.0 * math.pi))
    return 0.5 * near + 0.5 * far


def back_weight(diff, fog_sigma):
    near = jnp.exp(diff * diff * (-1.0 / (2.0 * SIGMA_BACK * SIGMA_BACK))) * (1.0 / (SIGMA_BACK * math.sqrt(2.0 * math.pi)))
    far = jnp.exp(diff * diff * (-1.0 / (2.0 * fog_sigma * fog_sigma))) * (1.0 / (fog_sigma * math.sqrt(2.0 * math.pi)))
    return 0.5 * near + 0.5 * far


def halves(value):
    high = value.astype(jnp.bfloat16)
    low = (value - high.astype(jnp.float32)).astype(jnp.bfloat16)
    return high, low


def kernel(
    axes, n, strips,
    pat_hbm, a1_ref, a2_ref, e1_ref, e2_ref, b_ref, kc_ref,
    dose_ref, expo_ref,
    pat, hp, hd, edge, xh, xl, yh, yl, fwd, d1, cs, msg, gath, wr, backs,
    load_sem, hp_send, hp_recv, hd_send, hd_recv, g_send, g_recv,
):
    rows, width = pat.shape
    cr, cc = rows // POOL, width // POOL
    fog_sigma = cr * n / 4.0
    me = lax.axis_index(axes[0]) * strips + lax.axis_index(axes[1])

    def place(index):
        return (index // strips, lax.rem(index, strips))

    barrier = pltpu.get_barrier_semaphore()

    def greet(k, carry):
        pl.semaphore_signal(barrier, inc=1, device_id=place(lax.rem(me + k, n)), device_id_type=MESH)
        return carry

    lax.fori_loop(1, n, greet, 0)
    loads = [
        pltpu.make_async_copy(pat_hbm.at[pl.ds(a * POOL, POOL)], pat.at[pl.ds(a * POOL, POOL)], load_sem.at[a])
        for a in range(cr)
    ]
    for load in loads:
        load.start()
    lane = lax.broadcasted_iota(jnp.int32, (n, LANES), 1)
    sender = lax.broadcasted_iota(jnp.int32, (n, LANES), 0)
    source = (sender * cr + lane // cc).astype(jnp.float32)
    for i in range(cr):
        diff = source - (me * cr + i).astype(jnp.float32)
        wr[i] = jnp.where(lane < cr * cc, back_weight(diff, fog_sigma), 0.0)
    zero_side = jnp.zeros((rows, LANES), jnp.bfloat16)
    for y in (yh, yl):
        y[:, 0:LANES] = zero_side
        y[:, LANES + width :] = zero_side

    def coarse_message(step):
        total = jnp.zeros((1, LANES), jnp.float32)
        for a in range(cr):
            for j in range(cc):
                cell = jnp.sum(cs[a, :, j * POOL : (j + 1) * POOL], axis=1, keepdims=True)
                cell = jnp.sum(cell, axis=0, keepdims=True)
                total = total + cell * kc_ref[a * cc + j : a * cc + j + 1, :]
        msg[step] = total
        gath[step, me] = total

    def gather_start(step):
        def one(k, carry):
            pltpu.make_async_remote_copy(
                src_ref=msg.at[step], dst_ref=gath.at[step, me],
                send_sem=g_send.at[step], recv_sem=g_recv.at[step],
                device_id=place(lax.rem(me + k, n)), device_id_type=MESH,
            ).start()
            return carry

        lax.fori_loop(1, n, one, 0)

    def gather_copy(step):
        part = gath.at[step, pl.ds(0, n - 1)]
        return pltpu.make_async_remote_copy(
            src_ref=part, dst_ref=part, send_sem=g_send.at[step], recv_sem=g_recv.at[step],
            device_id=place(lax.rem(me + 1, n)), device_id_type=MESH,
        )

    def backscatter(step):
        gather_copy(step).wait_recv()
        whole = gath[step][:, 0, :]
        for i in range(cr):
            mixed = jnp.sum(wr[i] * whole, axis=0, keepdims=True)
            cells = mixed[:, 0:cc]
            for a in range(1, cr):
                cells = cells + mixed[:, a * cc : (a + 1) * cc]
            cells = ETA_BACK * cells
            for j in range(cc):
                backs[i, :, j * POOL : (j + 1) * POOL] = jnp.broadcast_to(cells[:, j : j + 1], (8, POOL))

    def halo(src_of, buf, send, recv, up):
        peer = me - 1 if up else me + 1
        slot = 1 if up else 0
        return pltpu.make_async_remote_copy(
            src_ref=src_of(0 if up else 1), dst_ref=buf.at[slot],
            send_sem=send.at[slot], recv_sem=recv.at[slot],
            device_id=place(lax.rem(peer + n, n)), device_id_type=MESH,
        )

    has_before, has_after = me > 0, me < n - 1

    def pat_edge(side):
        return pat_hbm.at[pl.ds(0 if side == 0 else rows - H, H)]

    def edge_of(side):
        return edge.at[side]

    def halo_start(src_of, buf, send, recv):
        @pl.when(has_before)
        def _():
            halo(src_of, buf, send, recv, True).start()

        @pl.when(has_after)
        def _():
            halo(src_of, buf, send, recv, False).start()

    def halo_recv(src_of, buf, send, recv, use):
        @pl.when(has_before)
        def _():
            halo(src_of, buf, send, recv, False).wait_recv()
            use(0)

        @pl.when(has_after)
        def _():
            halo(src_of, buf, send, recv, True).wait_recv()
            use(1)

    def halo_sent(src_of, buf, send, recv):
        @pl.when(has_before)
        def _():
            halo(src_of, buf, send, recv, True).wait_send()

        @pl.when(has_after)
        def _():
            halo(src_of, buf, send, recv, False).wait_send()

    def level(p):
        return jnp.where(p == 1, 5.0, jnp.where(p == 2, 7.0, 0.0)).astype(jnp.float32)

    def store_rows(row, high, low, count):
        blk = pl.ds(pl.multiple_of(row, H), count)
        xh[blk, :] = high
        if low is not None:
            xl[blk, :] = low

    for side in range(2):
        at = 0 if side == 0 else rows + H
        xh[pl.ds(at, H), :] = jnp.zeros((H, width), jnp.bfloat16)
        xl[pl.ds(at, H), :] = jnp.zeros((H, width), jnp.bfloat16)

    cs[...] = jnp.zeros_like(cs)
    for a in range(cr):
        loads[a].wait()

        @pl.loop(0, POOL // H)
        def _(k):
            row = pl.multiple_of(a * POOL + k * H, H)
            value = level(pat[pl.ds(row, H), :])
            xh[pl.ds(row + H, H), :] = value.astype(jnp.bfloat16)
            cs[a] += value[0:8] + value[8:16]

    cs[...] = cs[...] * 0.2
    coarse_message(0)
    pl.semaphore_wait(barrier, n - 1)
    gather_start(0)
    halo_start(pat_edge, hp, hp_send, hp_recv)

    def row_blur(weights, first, cols, in_row, out_row, count):
        window = pl.ds(in_row, count + 2 * H)
        high = xh[window, cols]
        parts = [high, high] if first else [high, high, xl[window, cols]]
        value = jnp.dot(weights, jnp.concatenate(parts, axis=0), preferred_element_type=jnp.float32)
        return halves(value)

    def col_blur(out, j):
        window = pl.ds(pl.multiple_of(j * POOL, LANES), POOL + 2 * LANES)
        high, low = yh[out, window], yl[out, window]
        return jnp.dot(
            jnp.concatenate([high, high, low], axis=1), b_ref[...], preferred_element_type=jnp.float32
        )

    def inner_forward(first):
        a_ref = a1_ref if first else a2_ref

        @pl.loop(0, cc)
        def _(j):
            cols = pl.ds(pl.multiple_of(j * POOL, LANES), POOL)
            out_cols = pl.ds(pl.multiple_of(j * POOL + LANES, LANES), POOL)
            for t in range((rows - 2 * H) // TILE):
                high, low = row_blur(a_ref[...], first, cols, H + t * TILE, 0, TILE)
                out = pl.ds(H + t * TILE, TILE)
                yh[out, out_cols] = high
                yl[out, out_cols] = low

        @pl.loop(0, cc)
        def _(j):
            cols = pl.ds(pl.multiple_of(j * POOL, LANES), POOL)
            for t in range((rows - 2 * H) // TILE):
                out = pl.ds(H + t * TILE, TILE)
                fwd[out, cols] = col_blur(out, j)

    def edge_forward(first):
        e_ref = e1_ref if first else e2_ref

        @pl.loop(0, cc)
        def _(j):
            cols = pl.ds(pl.multiple_of(j * POOL, LANES), POOL)
            out_cols = pl.ds(pl.multiple_of(j * POOL + LANES, LANES), POOL)
            for row in (0, rows - H):
                high, low = row_blur(e_ref[...], first, cols, row, 0, H)
                yh[pl.ds(row, H), out_cols] = high
                yl[pl.ds(row, H), out_cols] = low

        @pl.loop(0, cc)
        def _(j):
            cols = pl.ds(pl.multiple_of(j * POOL, LANES), POOL)
            for row in (0, rows - H):
                out = pl.ds(row, H)
                fwd[out, cols] = col_blur(out, j)

    def exposed(blk, a):
        back = jnp.concatenate([backs[a], backs[a]], axis=0)
        return (fwd[blk, :] + back) * (1.0 / (1.0 + ETA_BACK))

    def first_update(row, a):
        blk = pl.ds(row, H)
        p = pat[blk, :]
        base = jnp.where(p == 1, 1.5, 1.95)
        dose = jnp.where(p > 0, base - exposed(blk, a), 0.0)
        high, low = halves(dose)
        d1[blk, :] = dose
        xh[pl.ds(row + H, H), :] = high
        xl[pl.ds(row + H, H), :] = low
        cs[a] += dose[0:8] + dose[8:16]
        return dose

    def last_update(row, a):
        blk = pl.ds(row, H)
        p = pat[blk, :]
        e = exposed(blk, a)
        target = jnp.where(p == 1, 0.5, 0.55)
        expo_ref[blk, :] = e
        dose_ref[blk, :] = jnp.where(p > 0, d1[blk, :] + target - e, 0.0)

    def inner_update(fn):
        for a in range(cr):
            low = H if a == 0 else 0
            high = POOL - H if a == cr - 1 else POOL

            @pl.loop(0, (high - low) // H)
            def _(k):
                fn(pl.multiple_of(a * POOL + low + k * H, H), a)

    inner_forward(True)
    backscatter(0)

    def use_pattern(slot):
        at = 0 if slot == 0 else rows + H
        xh[pl.ds(at, H), :] = level(hp[slot]).astype(jnp.bfloat16)

    halo_recv(pat_edge, hp, hp_send, hp_recv, use_pattern)
    edge_forward(True)
    cs[...] = jnp.zeros_like(cs)
    edge[0] = first_update(0, 0)
    edge[1] = first_update(rows - H, cr - 1)
    halo_start(edge_of, hd, hd_send, hd_recv)
    inner_update(first_update)
    coarse_message(1)
    gather_start(1)
    inner_forward(False)
    backscatter(1)
    inner_update(last_update)

    def use_dose(slot):
        at = 0 if slot == 0 else rows + H
        high, low = halves(hd[slot])
        xh[pl.ds(at, H), :] = high
        xl[pl.ds(at, H), :] = low

    halo_recv(edge_of, hd, hd_send, hd_recv, use_dose)
    edge_forward(False)
    last_update(0, 0)
    last_update(rows - H, cr - 1)
    halo_sent(pat_edge, hp, hp_send, hp_recv)
    halo_sent(edge_of, hd, hd_send, hd_recv)
    for step in range(2):
        gather_copy(step).wait_send()


def solution(mesh):
    axes = tuple(mesh.axis_names)
    strips = mesh.shape["strip"]
    n = strips * mesh.shape["band"]

    def local(pattern):
        rows, width = pattern.shape
        cr, cc = rows // POOL, width // POOL

        def wide(matrix, count):
            high, low = split(matrix)
            return np.concatenate([high, low, high][:count], axis=1)

        inner = band(TILE, TILE + 2 * H, 0)
        rim = band(H, 3 * H, 0)
        cols = band(POOL, POOL + 2 * LANES, LANES - H).T
        b_high, b_low = split(cols)
        kc = np.zeros((cr * cc, LANES), np.float32)
        for a in range(cr):
            for j in range(cc):
                kc[a * cc + j, a * cc : (a + 1) * cc] = back_np(
                    np.arange(cc) - float(j), cr * n / 4.0
                ) / (POOL * POOL)
        operands = (
            pattern,
            jnp.asarray(wide(inner / 5.0, 2)), jnp.asarray(wide(inner, 3)),
            jnp.asarray(wide(rim / 5.0, 2)), jnp.asarray(wide(rim, 3)),
            jnp.asarray(np.concatenate([b_high, b_low, b_high], axis=0)), jnp.asarray(kc),
        )
        vmem = pl.BlockSpec(memory_space=pltpu.VMEM)
        f32, bf16 = jnp.float32, jnp.bfloat16
        whole = jax.ShapeDtypeStruct((rows, width), f32)
        return pl.pallas_call(
            functools.partial(kernel, axes, n, strips),
            out_shape=(whole, whole),
            in_specs=[pl.BlockSpec(memory_space=pl.ANY)] + [vmem] * (len(operands) - 1),
            out_specs=(vmem, vmem),
            scratch_shapes=[
                pltpu.VMEM((rows, width), jnp.int32),
                pltpu.VMEM((2, H, width), jnp.int32),
                pltpu.VMEM((2, H, width), f32),
                pltpu.VMEM((2, H, width), f32),
                pltpu.VMEM((rows + 2 * H, width), bf16),
                pltpu.VMEM((rows + 2 * H, width), bf16),
                pltpu.VMEM((rows, width + 2 * LANES), bf16),
                pltpu.VMEM((rows, width + 2 * LANES), bf16),
                pltpu.VMEM((rows, width), f32),
                pltpu.VMEM((rows, width), f32),
                pltpu.VMEM((cr, 8, width), f32),
                pltpu.VMEM((2, 1, LANES), f32),
                pltpu.VMEM((2, n, 1, LANES), f32),
                pltpu.VMEM((cr, n, LANES), f32),
                pltpu.VMEM((cr, 8, width), f32),
                pltpu.SemaphoreType.DMA((cr,)),
                pltpu.SemaphoreType.DMA((2,)),
                pltpu.SemaphoreType.DMA((2,)),
                pltpu.SemaphoreType.DMA((2,)),
                pltpu.SemaphoreType.DMA((2,)),
                pltpu.SemaphoreType.DMA((2,)),
                pltpu.SemaphoreType.DMA((2,)),
            ],
            compiler_params=pltpu.CompilerParams(
                collective_id=0, has_side_effects=True, vmem_limit_bytes=48 * 1024 * 1024
            ),
            name="proximity",
        )(*operands)

    return jax.shard_map(
        local,
        mesh=mesh,
        in_specs=(P(("band", "strip"), None),),
        out_specs=(P(("band", "strip"), None), P(("band", "strip"), None)),
        check_vma=False,
    )
```

```python
import functools
import math

import jax
import jax.numpy as jnp
from jax import lax
from jax.experimental import pallas as pl
from jax.experimental.pallas import tpu as pltpu
from jax.sharding import PartitionSpec as P

POOL = 256
H = 16
ETA_BACK = 0.75
SIGMA_BACK = 6.0
TILE = 160
CHUNK = 32
CLEAR = 2.0**100
LANES = 128
MESH = pl.DeviceIdType.MESH


def taps_of(steps, scale):
    spread = H / 3.0
    total = sum(math.exp(-k * k / (2.0 * spread * spread)) for k in range(-H, H + 1))
    diff = steps.astype(jnp.float32)
    taps = jnp.exp(diff * diff * (-1.0 / (2.0 * spread * spread))) * (scale / total)
    return jnp.where(jnp.abs(steps) <= H, taps, 0.0)


def row_table(rows):
    depth = rows + 2 * H
    shape = (rows, 3 * depth)
    place = lax.broadcasted_iota(jnp.int32, shape, 1)
    second, third = place >= depth, place >= 2 * depth
    place = place - jnp.where(second, depth, 0) - jnp.where(third, depth, 0)
    taps = taps_of(place - H - lax.broadcasted_iota(jnp.int32, shape, 0), 1.0)
    high = taps.astype(jnp.bfloat16).astype(jnp.float32)
    low = jnp.logical_and(second, jnp.logical_not(third))
    return jnp.where(low, taps - high, high).astype(jnp.bfloat16)


def column_tables(scale):
    shape = (POOL, POOL)
    centre = taps_of(lax.broadcasted_iota(jnp.int32, shape, 0) - lax.broadcasted_iota(jnp.int32, shape, 1), scale)
    shape = (LANES, POOL)
    place = lax.broadcasted_iota(jnp.int32, shape, 0)
    place = jnp.where(place >= LANES // 2, place - LANES, place + POOL)
    rim = taps_of(place - lax.broadcasted_iota(jnp.int32, shape, 1), scale)
    return halves(centre) + halves(rim)


def back_weight(diff, fog_sigma):
    near = jnp.exp(diff * diff * (-1.0 / (2.0 * SIGMA_BACK * SIGMA_BACK))) * (1.0 / (SIGMA_BACK * math.sqrt(2.0 * math.pi)))
    far = jnp.exp(diff * diff * (-1.0 / (2.0 * fog_sigma * fog_sigma))) * (1.0 / (fog_sigma * math.sqrt(2.0 * math.pi)))
    return 0.5 * near + 0.5 * far


def halves(value):
    high = value.astype(jnp.bfloat16)
    low = (value - high.astype(jnp.float32)).astype(jnp.bfloat16)
    return high, low


def kernel(
    axes, n, strips,
    pat_hbm,
    fwd, base, backs,
    a_ref, e_ref, b1_ref, b2_ref, kc_ref,
    pat, hp, hd, edge, xh, xl, yh, yl, cs, msg, gath, wr,
    load_sem, hp_send, hp_recv, hd_send, hd_recv, g_send, g_recv,
):
    rows, width = pat.shape
    cr, cc = rows // POOL, width // POOL
    fog_sigma = cr * n / 4.0
    me = lax.axis_index(axes[0]) * strips + lax.axis_index(axes[1])

    def place(index):
        return (index // strips, lax.rem(index, strips))

    barrier = pltpu.get_barrier_semaphore()

    def greet(k, carry):
        pl.semaphore_signal(barrier, inc=1, device_id=place(lax.rem(me + k, n)), device_id_type=MESH)
        return carry

    lax.fori_loop(1, n, greet, 0)
    loads = [
        pltpu.make_async_copy(pat_hbm.at[pl.ds(a * POOL, POOL)], pat.at[pl.ds(a * POOL, POOL)], load_sem.at[a])
        for a in range(cr)
    ]
    for load in loads:
        load.start()
    a_ref[...] = row_table(TILE)
    e_ref[...] = row_table(H)
    for first, ref in ((True, b1_ref), (False, b2_ref)):
        c_high, c_low, r_high, r_low = column_tables(0.2 if first else 1.0)
        parts = [c_high, c_low, r_high, r_low] if first else [c_high, c_low, c_high, r_high, r_high, r_low]
        at = 0
        for part in parts:
            ref[at : at + part.shape[0], :] = part
            at += part.shape[0]
    spot_lane = lax.broadcasted_iota(jnp.int32, (H, LANES), 1)
    left_mask = jnp.where(spot_lane >= LANES // 2, 1.0, 0.0).astype(jnp.bfloat16)
    right_mask = jnp.where(spot_lane >= LANES // 2, 0.0, 1.0).astype(jnp.bfloat16)
    spot = lax.broadcasted_iota(jnp.int32, kc_ref.shape, 1) - lax.broadcasted_iota(jnp.int32, kc_ref.shape, 0)
    cell_row = lax.broadcasted_iota(jnp.int32, kc_ref.shape, 0) // cc
    same = lax.broadcasted_iota(jnp.int32, kc_ref.shape, 1) // cc == cell_row
    kc_ref[...] = jnp.where(same, back_weight(spot.astype(jnp.float32), fog_sigma) * (1.0 / (POOL * POOL)), 0.0)
    lane = lax.broadcasted_iota(jnp.int32, (n, LANES), 1)
    sender = lax.broadcasted_iota(jnp.int32, (n, LANES), 0)
    source = (sender * cr + lane // cc).astype(jnp.float32)
    for i in range(cr):
        diff = source - (me * cr + i).astype(jnp.float32)
        wr[i] = jnp.where(lane < cr * cc, back_weight(diff, fog_sigma), 0.0)
    zero_side = jnp.zeros((rows + 2 * H, LANES), jnp.bfloat16)
    for x in (xh, xl):
        x[:, 0:LANES] = zero_side
        x[:, LANES + width :] = zero_side

    def coarse_message(step):
        total = jnp.zeros((1, LANES), jnp.float32)
        for a in range(cr):
            for j in range(cc):
                cell = jnp.sum(cs[a, :, j * POOL : (j + 1) * POOL], axis=1, keepdims=True)
                cell = jnp.sum(cell, axis=0, keepdims=True)
                total = total + cell * kc_ref[a * cc + j : a * cc + j + 1, :]
        msg[step] = total
        gath[step, me] = total

    def gather_start(step):
        def one(k, carry):
            pltpu.make_async_remote_copy(
                src_ref=msg.at[step], dst_ref=gath.at[step, me],
                send_sem=g_send.at[step], recv_sem=g_recv.at[step],
                device_id=place(lax.rem(me + k, n)), device_id_type=MESH,
            ).start()
            return carry

        lax.fori_loop(1, n, one, 0)

    def gather_copy(step):
        part = gath.at[step, pl.ds(0, n - 1)]
        return pltpu.make_async_remote_copy(
            src_ref=part, dst_ref=part, send_sem=g_send.at[step], recv_sem=g_recv.at[step],
            device_id=place(lax.rem(me + 1, n)), device_id_type=MESH,
        )

    def backscatter(step):
        gather_copy(step).wait_recv()
        whole = gath[step][:, 0, :]
        for i in range(cr):
            mixed = jnp.sum(wr[i] * whole, axis=0, keepdims=True)
            cells = mixed[:, 0:cc]
            for a in range(1, cr):
                cells = cells + mixed[:, a * cc : (a + 1) * cc]
            cells = ETA_BACK * cells
            for j in range(cc):
                backs[i, :, j * POOL : (j + 1) * POOL] = jnp.broadcast_to(cells[:, j : j + 1], (8, POOL))

    def halo(src_of, buf, send, recv, up):
        peer = me - 1 if up else me + 1
        slot = 1 if up else 0
        return pltpu.make_async_remote_copy(
            src_ref=src_of(0 if up else 1), dst_ref=buf.at[slot],
            send_sem=send.at[slot], recv_sem=recv.at[slot],
            device_id=place(lax.rem(peer + n, n)), device_id_type=MESH,
        )

    has_before, has_after = me > 0, me < n - 1

    def pat_edge(side):
        return pat_hbm.at[pl.ds(0 if side == 0 else rows - H, H)]

    def edge_of(side):
        return edge.at[side]

    def halo_start(src_of, buf, send, recv):
        @pl.when(has_before)
        def _():
            halo(src_of, buf, send, recv, True).start()

        @pl.when(has_after)
        def _():
            halo(src_of, buf, send, recv, False).start()

    def halo_recv(src_of, buf, send, recv, use):
        @pl.when(has_before)
        def _():
            halo(src_of, buf, send, recv, False).wait_recv()
            use(0)

        @pl.when(has_after)
        def _():
            halo(src_of, buf, send, recv, True).wait_recv()
            use(1)

    def halo_sent(src_of, buf, send, recv):
        @pl.when(has_before)
        def _():
            halo(src_of, buf, send, recv, True).wait_send()

        @pl.when(has_after)
        def _():
            halo(src_of, buf, send, recv, False).wait_send()

    def level(p):
        return jnp.where(p == 1, 5.0, jnp.where(p == 2, 7.0, 0.0)).astype(jnp.float32)

    own = pl.ds(LANES, width)
    for side in range(2):
        at = 0 if side == 0 else rows + H
        xh[pl.ds(at, H), own] = jnp.zeros((H, width), jnp.bfloat16)
        xl[pl.ds(at, H), own] = jnp.zeros((H, width), jnp.bfloat16)

    cs[...] = jnp.zeros_like(cs)
    for a in range(cr):
        loads[a].wait()

        @pl.loop(0, POOL // H)
        def _(k):
            row = pl.multiple_of(a * POOL + k * H, H)
            value = level(pat[pl.ds(row, H), :])
            xh[pl.ds(row + H, H), own] = value.astype(jnp.bfloat16)
            cs[a] += value[0:8] + value[8:16]

    cs[...] = cs[...] * 0.2
    coarse_message(0)
    pl.semaphore_wait(barrier, n - 1)
    gather_start(0)
    halo_start(pat_edge, hp, hp_send, hp_recv)

    def tile_cols(j, offset, count):
        return pl.ds(pl.multiple_of(j * POOL + offset, LANES), count)

    def window(ref, spans, cols):
        return jnp.concatenate([ref[pl.ds(at, count), cols] for at, count in spans], axis=0)

    def col_blur(first, j, spans):
        def rim(ref):
            count = sum(c for _, c in spans)
            left = window(ref, spans, tile_cols(j, 0, LANES))
            right = window(ref, spans, tile_cols(j, LANES + POOL, LANES))
            times = (count // H, 1)
            return left * jnp.tile(left_mask, times) + right * jnp.tile(right_mask, times)

        centre = tile_cols(j, LANES, POOL)
        high, rim_high = window(xh, spans, centre), rim(xh)
        if first:
            parts, table = [high, high, rim_high, rim_high], b1_ref
        else:
            parts, table = [high, high, window(xl, spans, centre), rim_high, rim(xl), rim_high], b2_ref
        value = jnp.dot(jnp.concatenate(parts, axis=1), table[...], preferred_element_type=jnp.float32)
        value_high, value_low = halves(value)
        done = 0
        for at, count in spans:
            yh[pl.ds(at, count), tile_cols(j, 0, POOL)] = value_high[done : done + count]
            yl[pl.ds(at, count), tile_cols(j, 0, POOL)] = value_low[done : done + count]
            done += count

    def row_blur(weights, j, row, count):
        cols = tile_cols(j, 0, POOL)
        high = yh[pl.ds(row, count + 2 * H), cols]
        low = yl[pl.ds(row, count + 2 * H), cols]
        return jnp.dot(weights[...], jnp.concatenate([high, high, low], axis=0), preferred_element_type=jnp.float32)

    def each_tile(fn, unroll):
        @pl.loop(0, cc // unroll)
        def _(k):
            for u in range(unroll):
                fn(k * unroll + u)

    def first_update(value, row, count, j):
        cols = tile_cols(j, 0, POOL)
        at = row
        while at < row + count:
            a = at // POOL
            part = min(row + count, (a + 1) * POOL) - at
            blk = pl.ds(at, part)
            p = pat[blk, cols]
            back = jnp.tile(backs[a, :, cols], (part // 8, 1))
            e = (value[at - row : at - row + part] + back) * (1.0 / (1.0 + ETA_BACK))
            dose = jnp.where(p > 0, jnp.where(p == 1, 1.5, 1.95) - e, 0.0)
            high, low = halves(dose)
            base[blk, cols] = jnp.where(p > 0, dose + jnp.where(p == 1, 0.5, 0.55), CLEAR)
            inside = tile_cols(j, LANES, POOL)
            xh[pl.ds(at + H, part), inside] = high
            xl[pl.ds(at + H, part), inside] = low
            cs[a, :, cols] += jnp.sum(dose.reshape(part // 8, 8, POOL), axis=0)
            if row == 0:
                edge[0, :, cols] = dose
            if row == rows - H:
                edge[1, :, cols] = dose
            at += part

    def last_store(value, row, count, j):
        fwd[pl.ds(row, count), tile_cols(j, 0, POOL)] = value

    def inner_rows(use):
        def one(j):
            for row in range(H, rows - H, TILE):
                use(row_blur(a_ref, j, row, TILE), row, TILE, j)

        each_tile(one, 2)

    def edge_rows(first, use):
        spans = ((0, H), (rows + H, H))
        each_tile(lambda j: col_blur(first, j, spans), 4)

        def one(j):
            for row in (0, rows - H):
                use(row_blur(e_ref, j, row, H), row, H, j)

        each_tile(one, 4)

    each_tile(lambda j: col_blur(True, j, ((H, rows),)), 2)
    cs[...] = jnp.zeros_like(cs)
    backscatter(0)
    inner_rows(first_update)

    def use_pattern(slot):
        at = 0 if slot == 0 else rows + H
        xh[pl.ds(at, H), own] = level(hp[slot]).astype(jnp.bfloat16)

    halo_recv(pat_edge, hp, hp_send, hp_recv, use_pattern)
    edge_rows(True, first_update)
    halo_start(edge_of, hd, hd_send, hd_recv)
    coarse_message(1)
    gather_start(1)
    each_tile(lambda j: col_blur(False, j, ((H, rows),)), 2)
    inner_rows(last_store)
    backscatter(1)

    def use_dose(slot):
        at = 0 if slot == 0 else rows + H
        high, low = halves(hd[slot])
        xh[pl.ds(at, H), own] = high
        xl[pl.ds(at, H), own] = low

    halo_recv(edge_of, hd, hd_send, hd_recv, use_dose)
    edge_rows(False, last_store)
    halo_sent(pat_edge, hp, hp_send, hp_recv)
    halo_sent(edge_of, hd, hd_send, hd_recv)
    for step in range(2):
        gather_copy(step).wait_send()


def finish_kernel(fwd, base, backs, dose_hbm, expo_hbm, dose, expo, sem):
    rows = fwd.shape[0]
    steps = rows // CHUNK

    def copies(k):
        blk = pl.ds(pl.multiple_of(k * CHUNK, CHUNK), CHUNK)
        return [
            pltpu.make_async_copy(src.at[blk], dst.at[blk], sem.at[i, k])
            for i, (src, dst) in enumerate(((dose, dose_hbm), (expo, expo_hbm)))
        ]

    for a in range(rows // POOL):

        @pl.loop(0, POOL // CHUNK)
        def _(k):
            step = a * (POOL // CHUNK) + k
            for r in range(0, CHUNK, 8):
                blk = pl.ds(pl.multiple_of(step * CHUNK + r, 8), 8)
                e = (fwd[blk, :] + backs[a]) * (1.0 / (1.0 + ETA_BACK))
                u = base[blk, :]
                expo[blk, :] = e
                dose[blk, :] = jnp.where(u == CLEAR, 0.0, u - e)
            for copy in copies(step):
                copy.start()

    @pl.loop(0, steps)
    def _(k):
        for copy in copies(k):
            copy.wait()


def solution(mesh):
    axes = tuple(mesh.axis_names)
    strips = mesh.shape["strip"]
    n = strips * mesh.shape["band"]

    def local(pattern):
        rows, width = pattern.shape
        cr, cc = rows // POOL, width // POOL

        vmem = pl.BlockSpec(memory_space=pltpu.VMEM)
        f32, bf16 = jnp.float32, jnp.bfloat16
        whole = jax.ShapeDtypeStruct((rows, width), f32)
        hbm = pl.BlockSpec(memory_space=pltpu.HBM)
        fwd, base, backs = pl.pallas_call(
            functools.partial(kernel, axes, n, strips),
            out_shape=(whole, whole, jax.ShapeDtypeStruct((cr, 8, width), f32)),
            in_specs=[hbm],
            out_specs=(vmem, vmem, vmem),
            scratch_shapes=[
                pltpu.VMEM((TILE, 3 * (TILE + 2 * H)), bf16),
                pltpu.VMEM((H, 3 * 3 * H), bf16),
                pltpu.VMEM((2 * (POOL + LANES), POOL), bf16),
                pltpu.VMEM((3 * (POOL + LANES), POOL), bf16),
                pltpu.VMEM((cr * cc, LANES), f32),
                pltpu.VMEM((rows, width), jnp.int32),
                pltpu.VMEM((2, H, width), jnp.int32),
                pltpu.VMEM((2, H, width), f32),
                pltpu.VMEM((2, H, width), f32),
                pltpu.VMEM((rows + 2 * H, width + 2 * LANES), bf16),
                pltpu.VMEM((rows + 2 * H, width + 2 * LANES), bf16),
                pltpu.VMEM((rows + 2 * H, width), bf16),
                pltpu.VMEM((rows + 2 * H, width), bf16),
                pltpu.VMEM((cr, 8, width), f32),
                pltpu.VMEM((2, 1, LANES), f32),
                pltpu.VMEM((2, n, 1, LANES), f32),
                pltpu.VMEM((cr, n, LANES), f32),
                pltpu.SemaphoreType.DMA((cr,)),
                pltpu.SemaphoreType.DMA((2,)),
                pltpu.SemaphoreType.DMA((2,)),
                pltpu.SemaphoreType.DMA((2,)),
                pltpu.SemaphoreType.DMA((2,)),
                pltpu.SemaphoreType.DMA((2,)),
                pltpu.SemaphoreType.DMA((2,)),
            ],
            compiler_params=pltpu.CompilerParams(
                collective_id=0, has_side_effects=True, vmem_limit_bytes=44 * 1024 * 1024
            ),
            name="proximity",
        )(pattern)
        return pl.pallas_call(
            finish_kernel,
            out_shape=(whole, whole),
            in_specs=[vmem] * 3,
            out_specs=(hbm, hbm),
            scratch_shapes=[
                pltpu.VMEM((rows, width), f32),
                pltpu.VMEM((rows, width), f32),
                pltpu.SemaphoreType.DMA((2, rows // CHUNK)),
            ],
            compiler_params=pltpu.CompilerParams(vmem_limit_bytes=20 * 1024 * 1024),
            name="finish",
        )(fwd, base, backs)

    return jax.shard_map(
        local,
        mesh=mesh,
        in_specs=(P(("band", "strip"), None),),
        out_specs=(P(("band", "strip"), None), P(("band", "strip"), None)),
        check_vma=False,
    )
```

```python
import functools
import math

import jax
import jax.numpy as jnp
from jax import lax
from jax.experimental import pallas as pl
from jax.experimental.pallas import tpu as pltpu
from jax.sharding import PartitionSpec as P

POOL = 256
H = 16
ETA_BACK = 0.75
SIGMA_BACK = 6.0
TILE = 160
CHUNK = 32
CLEAR = 2.0**100
LANES = 128
MESH = pl.DeviceIdType.MESH


def taps_of(steps, scale):
    spread = H / 3.0
    total = sum(math.exp(-k * k / (2.0 * spread * spread)) for k in range(-H, H + 1))
    diff = steps.astype(jnp.float32)
    taps = jnp.exp(diff * diff * (-1.0 / (2.0 * spread * spread))) * (scale / total)
    return jnp.where(jnp.abs(steps) <= H, taps, 0.0)


def row_table(rows):
    depth = rows + 2 * H
    shape = (rows, 3 * depth)
    place = lax.broadcasted_iota(jnp.int32, shape, 1)
    second, third = place >= depth, place >= 2 * depth
    place = place - jnp.where(second, depth, 0) - jnp.where(third, depth, 0)
    taps = taps_of(place - H - lax.broadcasted_iota(jnp.int32, shape, 0), 1.0)
    high = taps.astype(jnp.bfloat16).astype(jnp.float32)
    low = jnp.logical_and(second, jnp.logical_not(third))
    return jnp.where(low, taps - high, high).astype(jnp.bfloat16)


def column_tables(scale):
    shape = (POOL, POOL)
    centre = taps_of(lax.broadcasted_iota(jnp.int32, shape, 0) - lax.broadcasted_iota(jnp.int32, shape, 1), scale)
    shape = (LANES, POOL)
    place = lax.broadcasted_iota(jnp.int32, shape, 0)
    place = jnp.where(place >= LANES // 2, place - LANES, place + POOL)
    rim = taps_of(place - lax.broadcasted_iota(jnp.int32, shape, 1), scale)
    return halves(centre) + halves(rim)


def back_weight(diff, fog_sigma):
    near = jnp.exp(diff * diff * (-1.0 / (2.0 * SIGMA_BACK * SIGMA_BACK))) * (1.0 / (SIGMA_BACK * math.sqrt(2.0 * math.pi)))
    far = jnp.exp(diff * diff * (-1.0 / (2.0 * fog_sigma * fog_sigma))) * (1.0 / (fog_sigma * math.sqrt(2.0 * math.pi)))
    return 0.5 * near + 0.5 * far


def halves(value):
    high = value.astype(jnp.bfloat16)
    low = (value - high.astype(jnp.float32)).astype(jnp.bfloat16)
    return high, low


def kernel(
    axes, n, strips,
    pat_hbm,
    fwd, base, backs,
    a_ref, e_ref, b1_ref, b2_ref, kc_ref,
    pat, hp, hd, edge, xh, xl, yh, yl, cs, msg, gath, wr,
    load_sem, hp_send, hp_recv, hd_send, hd_recv, g_send, g_recv,
):
    rows, width = pat.shape
    cr, cc = rows // POOL, width // POOL
    fog_sigma = cr * n / 4.0
    me = lax.axis_index(axes[0]) * strips + lax.axis_index(axes[1])

    def place(index):
        return (index // strips, lax.rem(index, strips))

    barrier = pltpu.get_barrier_semaphore()

    def greet(k, carry):
        pl.semaphore_signal(barrier, inc=1, device_id=place(lax.rem(me + k, n)), device_id_type=MESH)
        return carry

    lax.fori_loop(1, n, greet, 0)
    loads = [
        pltpu.make_async_copy(pat_hbm.at[pl.ds(a * POOL, POOL)], pat.at[pl.ds(a * POOL, POOL)], load_sem.at[a])
        for a in range(cr)
    ]
    for load in loads:
        load.start()
    a_ref[...] = row_table(TILE)
    e_ref[...] = row_table(H)
    for first, ref in ((True, b1_ref), (False, b2_ref)):
        c_high, c_low, r_high, r_low = column_tables(0.2 if first else 1.0)
        parts = [c_high, c_low, r_high, r_low] if first else [c_high, c_low, c_high, r_high, r_high, r_low]
        at = 0
        for part in parts:
            ref[at : at + part.shape[0], :] = part
            at += part.shape[0]
    spot_lane = lax.broadcasted_iota(jnp.int32, (H, LANES), 1)
    left_mask = jnp.where(spot_lane >= LANES // 2, 1.0, 0.0).astype(jnp.bfloat16)
    right_mask = jnp.where(spot_lane >= LANES // 2, 0.0, 1.0).astype(jnp.bfloat16)
    spot = lax.broadcasted_iota(jnp.int32, kc_ref.shape, 1) - lax.broadcasted_iota(jnp.int32, kc_ref.shape, 0)
    cell_row = lax.broadcasted_iota(jnp.int32, kc_ref.shape, 0) // cc
    same = lax.broadcasted_iota(jnp.int32, kc_ref.shape, 1) // cc == cell_row
    kc_ref[...] = jnp.where(same, back_weight(spot.astype(jnp.float32), fog_sigma) * (1.0 / (POOL * POOL)), 0.0)
    lane = lax.broadcasted_iota(jnp.int32, (n, LANES), 1)
    sender = lax.broadcasted_iota(jnp.int32, (n, LANES), 0)
    source = (sender * cr + lane // cc).astype(jnp.float32)
    for i in range(cr):
        diff = source - (me * cr + i).astype(jnp.float32)
        wr[i] = jnp.where(lane < cr * cc, back_weight(diff, fog_sigma), 0.0)
    zero_side = jnp.zeros((rows + 2 * H, LANES), jnp.bfloat16)
    for x in (xh, xl):
        x[:, 0:LANES] = zero_side
        x[:, LANES + width :] = zero_side

    def coarse_message(step):
        total = jnp.zeros((1, LANES), jnp.float32)
        for a in range(cr):
            for j in range(cc):
                cell = jnp.sum(cs[a, :, j * POOL : (j + 1) * POOL], axis=1, keepdims=True)
                cell = jnp.sum(cell, axis=0, keepdims=True)
                total = total + cell * kc_ref[a * cc + j : a * cc + j + 1, :]
        msg[step] = total
        gath[step, me] = total

    def gather_start(step):
        def one(k, carry):
            pltpu.make_async_remote_copy(
                src_ref=msg.at[step], dst_ref=gath.at[step, me],
                send_sem=g_send.at[step], recv_sem=g_recv.at[step],
                device_id=place(lax.rem(me + k, n)), device_id_type=MESH,
            ).start()
            return carry

        lax.fori_loop(1, n, one, 0)

    def gather_copy(step):
        part = gath.at[step, pl.ds(0, n - 1)]
        return pltpu.make_async_remote_copy(
            src_ref=part, dst_ref=part, send_sem=g_send.at[step], recv_sem=g_recv.at[step],
            device_id=place(lax.rem(me + 1, n)), device_id_type=MESH,
        )

    def backscatter(step):
        gather_copy(step).wait_recv()
        whole = gath[step][:, 0, :]
        for i in range(cr):
            mixed = jnp.sum(wr[i] * whole, axis=0, keepdims=True)
            cells = mixed[:, 0:cc]
            for a in range(1, cr):
                cells = cells + mixed[:, a * cc : (a + 1) * cc]
            cells = ETA_BACK * cells
            for j in range(cc):
                backs[i, :, j * POOL : (j + 1) * POOL] = jnp.broadcast_to(cells[:, j : j + 1], (8, POOL))

    def halo(src_of, buf, send, recv, up):
        peer = me - 1 if up else me + 1
        slot = 1 if up else 0
        return pltpu.make_async_remote_copy(
            src_ref=src_of(0 if up else 1), dst_ref=buf.at[slot],
            send_sem=send.at[slot], recv_sem=recv.at[slot],
            device_id=place(lax.rem(peer + n, n)), device_id_type=MESH,
        )

    has_before, has_after = me > 0, me < n - 1

    def pat_edge(side):
        return pat_hbm.at[pl.ds(0 if side == 0 else rows - H, H)]

    def edge_of(side):
        return edge.at[side]

    my_strip = lax.axis_index(axes[1])
    first_strip, last_strip = my_strip == 0, my_strip == strips - 1

    def halo_start(src_of, buf, send, recv, far):
        before = first_strip if far else jnp.logical_not(first_strip)
        after = last_strip if far else jnp.logical_not(last_strip)

        @pl.when(jnp.logical_and(has_before, before))
        def _():
            halo(src_of, buf, send, recv, True).start()

        @pl.when(jnp.logical_and(has_after, after))
        def _():
            halo(src_of, buf, send, recv, False).start()

    def halo_recv(src_of, buf, send, recv, use):
        @pl.when(has_before)
        def _():
            halo(src_of, buf, send, recv, False).wait_recv()
            use(0)

        @pl.when(has_after)
        def _():
            halo(src_of, buf, send, recv, True).wait_recv()
            use(1)

    def halo_sent(src_of, buf, send, recv):
        @pl.when(has_before)
        def _():
            halo(src_of, buf, send, recv, True).wait_send()

        @pl.when(has_after)
        def _():
            halo(src_of, buf, send, recv, False).wait_send()

    def level(p):
        return jnp.where(p == 1, 5.0, jnp.where(p == 2, 7.0, 0.0)).astype(jnp.float32)

    own = pl.ds(LANES, width)
    for side in range(2):
        at = 0 if side == 0 else rows + H
        xh[pl.ds(at, H), own] = jnp.zeros((H, width), jnp.bfloat16)
        xl[pl.ds(at, H), own] = jnp.zeros((H, width), jnp.bfloat16)

    cs[...] = jnp.zeros_like(cs)
    for a in range(cr):
        loads[a].wait()

        @pl.loop(0, POOL // H)
        def _(k):
            row = pl.multiple_of(a * POOL + k * H, H)
            value = level(pat[pl.ds(row, H), :])
            xh[pl.ds(row + H, H), own] = value.astype(jnp.bfloat16)
            cs[a] += value[0:8] + value[8:16]

    cs[...] = cs[...] * 0.2
    coarse_message(0)
    pl.semaphore_wait(barrier, n - 1)
    halo_start(pat_edge, hp, hp_send, hp_recv, True)
    gather_start(0)

    def tile_cols(j, offset, count):
        return pl.ds(pl.multiple_of(j * POOL + offset, LANES), count)

    def window(ref, spans, cols):
        return jnp.concatenate([ref[pl.ds(at, count), cols] for at, count in spans], axis=0)

    def col_blur(first, j, spans):
        def rim(ref):
            count = sum(c for _, c in spans)
            left = window(ref, spans, tile_cols(j, 0, LANES))
            right = window(ref, spans, tile_cols(j, LANES + POOL, LANES))
            times = (count // H, 1)
            return left * jnp.tile(left_mask, times) + right * jnp.tile(right_mask, times)

        centre = tile_cols(j, LANES, POOL)
        high, rim_high = window(xh, spans, centre), rim(xh)
        if first:
            parts, table = [high, high, rim_high, rim_high], b1_ref
        else:
            parts, table = [high, high, window(xl, spans, centre), rim_high, rim(xl), rim_high], b2_ref
        value = jnp.dot(jnp.concatenate(parts, axis=1), table[...], preferred_element_type=jnp.float32)
        value_high, value_low = halves(value)
        done = 0
        for at, count in spans:
            yh[pl.ds(at, count), tile_cols(j, 0, POOL)] = value_high[done : done + count]
            yl[pl.ds(at, count), tile_cols(j, 0, POOL)] = value_low[done : done + count]
            done += count

    def row_blur(weights, j, row, count):
        cols = tile_cols(j, 0, POOL)
        high = yh[pl.ds(row, count + 2 * H), cols]
        low = yl[pl.ds(row, count + 2 * H), cols]
        return jnp.dot(weights[...], jnp.concatenate([high, high, low], axis=0), preferred_element_type=jnp.float32)

    def each_tile(fn, unroll):
        @pl.loop(0, cc // unroll)
        def _(k):
            for u in range(unroll):
                fn(k * unroll + u)

    def first_update(value, row, count, j):
        cols = tile_cols(j, 0, POOL)
        at = row
        while at < row + count:
            a = at // POOL
            part = min(row + count, (a + 1) * POOL) - at
            blk = pl.ds(at, part)
            p = pat[blk, cols]
            back = jnp.tile(backs[a, :, cols], (part // 8, 1))
            e = (value[at - row : at - row + part] + back) * (1.0 / (1.0 + ETA_BACK))
            dose = jnp.where(p > 0, jnp.where(p == 1, 1.5, 1.95) - e, 0.0)
            high, low = halves(dose)
            base[blk, cols] = jnp.where(p > 0, dose + jnp.where(p == 1, 0.5, 0.55), CLEAR)
            inside = tile_cols(j, LANES, POOL)
            xh[pl.ds(at + H, part), inside] = high
            xl[pl.ds(at + H, part), inside] = low
            cs[a, :, cols] += jnp.sum(dose.reshape(part // 8, 8, POOL), axis=0)
            if row == 0:
                edge[0, :, cols] = dose
            if row == rows - H:
                edge[1, :, cols] = dose
            at += part

    def last_store(value, row, count, j):
        fwd[pl.ds(row, count), tile_cols(j, 0, POOL)] = value

    def inner_rows(use):
        def one(j):
            for row in range(H, rows - H, TILE):
                use(row_blur(a_ref, j, row, TILE), row, TILE, j)

        each_tile(one, 2)

    def edge_rows(first, use):
        spans = ((0, H), (rows + H, H))
        each_tile(lambda j: col_blur(first, j, spans), 4)

        def one(j):
            for row in (0, rows - H):
                use(row_blur(e_ref, j, row, H), row, H, j)

        each_tile(one, 4)

    each_tile(lambda j: col_blur(True, j, ((H, rows),)), 2)
    halo_start(pat_edge, hp, hp_send, hp_recv, False)
    cs[...] = jnp.zeros_like(cs)
    backscatter(0)
    inner_rows(first_update)

    def use_pattern(slot):
        at = 0 if slot == 0 else rows + H
        xh[pl.ds(at, H), own] = level(hp[slot]).astype(jnp.bfloat16)

    halo_recv(pat_edge, hp, hp_send, hp_recv, use_pattern)
    edge_rows(True, first_update)
    halo_start(edge_of, hd, hd_send, hd_recv, True)
    coarse_message(1)
    gather_start(1)
    each_tile(lambda j: col_blur(False, j, ((H, rows),)), 2)
    halo_start(edge_of, hd, hd_send, hd_recv, False)
    inner_rows(last_store)
    backscatter(1)

    def use_dose(slot):
        at = 0 if slot == 0 else rows + H
        high, low = halves(hd[slot])
        xh[pl.ds(at, H), own] = high
        xl[pl.ds(at, H), own] = low

    halo_recv(edge_of, hd, hd_send, hd_recv, use_dose)
    edge_rows(False, last_store)
    halo_sent(pat_edge, hp, hp_send, hp_recv)
    halo_sent(edge_of, hd, hd_send, hd_recv)
    for step in range(2):
        gather_copy(step).wait_send()


def finish_kernel(fwd, base, backs, dose_hbm, expo_hbm, dose, expo, sem):
    rows = fwd.shape[0]
    steps = rows // CHUNK

    def copies(k):
        blk = pl.ds(pl.multiple_of(k * CHUNK, CHUNK), CHUNK)
        return [
            pltpu.make_async_copy(src.at[blk], dst.at[blk], sem.at[i, k])
            for i, (src, dst) in enumerate(((dose, dose_hbm), (expo, expo_hbm)))
        ]

    for a in range(rows // POOL):

        @pl.loop(0, POOL // CHUNK)
        def _(k):
            step = a * (POOL // CHUNK) + k
            for r in range(0, CHUNK, 8):
                blk = pl.ds(pl.multiple_of(step * CHUNK + r, 8), 8)
                e = (fwd[blk, :] + backs[a]) * (1.0 / (1.0 + ETA_BACK))
                u = base[blk, :]
                expo[blk, :] = e
                dose[blk, :] = jnp.where(u == CLEAR, 0.0, u - e)
            for copy in copies(step):
                copy.start()

    @pl.loop(0, steps)
    def _(k):
        for copy in copies(k):
            copy.wait()


def solution(mesh):
    axes = tuple(mesh.axis_names)
    strips = mesh.shape["strip"]
    n = strips * mesh.shape["band"]

    def local(pattern):
        rows, width = pattern.shape
        cr, cc = rows // POOL, width // POOL

        vmem = pl.BlockSpec(memory_space=pltpu.VMEM)
        f32, bf16 = jnp.float32, jnp.bfloat16
        whole = jax.ShapeDtypeStruct((rows, width), f32)
        hbm = pl.BlockSpec(memory_space=pltpu.HBM)
        fwd, base, backs = pl.pallas_call(
            functools.partial(kernel, axes, n, strips),
            out_shape=(whole, whole, jax.ShapeDtypeStruct((cr, 8, width), f32)),
            in_specs=[hbm],
            out_specs=(vmem, vmem, vmem),
            scratch_shapes=[
                pltpu.VMEM((TILE, 3 * (TILE + 2 * H)), bf16),
                pltpu.VMEM((H, 3 * 3 * H), bf16),
                pltpu.VMEM((2 * (POOL + LANES), POOL), bf16),
                pltpu.VMEM((3 * (POOL + LANES), POOL), bf16),
                pltpu.VMEM((cr * cc, LANES), f32),
                pltpu.VMEM((rows, width), jnp.int32),
                pltpu.VMEM((2, H, width), jnp.int32),
                pltpu.VMEM((2, H, width), f32),
                pltpu.VMEM((2, H, width), f32),
                pltpu.VMEM((rows + 2 * H, width + 2 * LANES), bf16),
                pltpu.VMEM((rows + 2 * H, width + 2 * LANES), bf16),
                pltpu.VMEM((rows + 2 * H, width), bf16),
                pltpu.VMEM((rows + 2 * H, width), bf16),
                pltpu.VMEM((cr, 8, width), f32),
                pltpu.VMEM((2, 1, LANES), f32),
                pltpu.VMEM((2, n, 1, LANES), f32),
                pltpu.VMEM((cr, n, LANES), f32),
                pltpu.SemaphoreType.DMA((cr,)),
                pltpu.SemaphoreType.DMA((2,)),
                pltpu.SemaphoreType.DMA((2,)),
                pltpu.SemaphoreType.DMA((2,)),
                pltpu.SemaphoreType.DMA((2,)),
                pltpu.SemaphoreType.DMA((2,)),
                pltpu.SemaphoreType.DMA((2,)),
            ],
            compiler_params=pltpu.CompilerParams(
                collective_id=0, has_side_effects=True, vmem_limit_bytes=44 * 1024 * 1024
            ),
            name="proximity",
        )(pattern)
        return pl.pallas_call(
            finish_kernel,
            out_shape=(whole, whole),
            in_specs=[vmem] * 3,
            out_specs=(hbm, hbm),
            scratch_shapes=[
                pltpu.VMEM((rows, width), f32),
                pltpu.VMEM((rows, width), f32),
                pltpu.SemaphoreType.DMA((2, rows // CHUNK)),
            ],
            compiler_params=pltpu.CompilerParams(vmem_limit_bytes=20 * 1024 * 1024),
            name="finish",
        )(fwd, base, backs)

    return jax.shard_map(
        local,
        mesh=mesh,
        in_specs=(P(("band", "strip"), None),),
        out_specs=(P(("band", "strip"), None), P(("band", "strip"), None)),
        check_vma=False,
    )
```

```python
import functools
import math

import jax
import jax.numpy as jnp
from jax import lax
from jax.experimental import pallas as pl
from jax.experimental.pallas import tpu as pltpu
from jax.sharding import PartitionSpec as P

POOL = 256
H = 16
ETA_BACK = 0.75
SIGMA_BACK = 6.0
TILE = 160
CHUNK = 32
CLEAR = 2.0**100
LANES = 128
MESH = pl.DeviceIdType.MESH


def taps_of(steps, scale):
    spread = H / 3.0
    total = sum(math.exp(-k * k / (2.0 * spread * spread)) for k in range(-H, H + 1))
    diff = steps.astype(jnp.float32)
    taps = jnp.exp(diff * diff * (-1.0 / (2.0 * spread * spread))) * (scale / total)
    return jnp.where(jnp.abs(steps) <= H, taps, 0.0)


def row_table(rows):
    depth = rows + 2 * H
    shape = (rows, 3 * depth)
    place = lax.broadcasted_iota(jnp.int32, shape, 1)
    second, third = place >= depth, place >= 2 * depth
    place = place - jnp.where(second, depth, 0) - jnp.where(third, depth, 0)
    taps = taps_of(place - H - lax.broadcasted_iota(jnp.int32, shape, 0), 1.0)
    high = taps.astype(jnp.bfloat16).astype(jnp.float32)
    low = jnp.logical_and(second, jnp.logical_not(third))
    return jnp.where(low, taps - high, high).astype(jnp.bfloat16)


def column_tables(scale):
    shape = (POOL, POOL)
    centre = taps_of(lax.broadcasted_iota(jnp.int32, shape, 0) - lax.broadcasted_iota(jnp.int32, shape, 1), scale)
    shape = (LANES, POOL)
    place = lax.broadcasted_iota(jnp.int32, shape, 0)
    place = jnp.where(place >= LANES // 2, place - LANES, place + POOL)
    rim = taps_of(place - lax.broadcasted_iota(jnp.int32, shape, 1), scale)
    return halves(centre) + halves(rim)


def back_weight(diff, fog_sigma):
    near = jnp.exp(diff * diff * (-1.0 / (2.0 * SIGMA_BACK * SIGMA_BACK))) * (1.0 / (SIGMA_BACK * math.sqrt(2.0 * math.pi)))
    far = jnp.exp(diff * diff * (-1.0 / (2.0 * fog_sigma * fog_sigma))) * (1.0 / (fog_sigma * math.sqrt(2.0 * math.pi)))
    return 0.5 * near + 0.5 * far


def halves(value):
    high = value.astype(jnp.bfloat16)
    low = (value - high.astype(jnp.float32)).astype(jnp.bfloat16)
    return high, low


def kernel(
    axes, n, strips,
    pat_hbm,
    fwd, base, backs,
    a_ref, e_ref, b1_ref, b2_ref, kc_ref,
    pat, hp, hd, edge, xh, xl, yh, yl, cs, msg, gath, wr,
    load_sem, hp_send, hp_recv, hd_send, hd_recv, g_send, g_recv,
):
    rows, width = pat.shape
    cr, cc = rows // POOL, width // POOL
    fog_sigma = cr * n / 4.0
    me = lax.axis_index(axes[0]) * strips + lax.axis_index(axes[1])

    def place(index):
        return (lax.div(index, strips), lax.rem(index, strips))

    stride = max(d for d in range(1, 33) if (n - 1) % d == 0)

    def each_peer(fn):
        @pl.loop(0, (n - 1) // stride)
        def _(k):
            for u in range(stride):
                peer = me + (k * stride + u + 1)
                fn(place(jnp.where(peer >= n, peer - n, peer)))


    barrier = pltpu.get_barrier_semaphore()

    each_peer(lambda peer: pl.semaphore_signal(barrier, inc=1, device_id=peer, device_id_type=MESH))
    loads = [
        pltpu.make_async_copy(pat_hbm.at[pl.ds(a * POOL, POOL)], pat.at[pl.ds(a * POOL, POOL)], load_sem.at[a])
        for a in range(cr)
    ]
    for load in loads:
        load.start()
    a_ref[...] = row_table(TILE)
    e_ref[...] = row_table(H)
    for first, ref in ((True, b1_ref), (False, b2_ref)):
        c_high, c_low, r_high, r_low = column_tables(0.2 if first else 1.0)
        parts = [c_high, c_low, r_high, r_low] if first else [c_high, c_low, c_high, r_high, r_high, r_low]
        at = 0
        for part in parts:
            ref[at : at + part.shape[0], :] = part
            at += part.shape[0]
    spot_lane = lax.broadcasted_iota(jnp.int32, (H, LANES), 1)
    left_mask = jnp.where(spot_lane >= LANES // 2, 1.0, 0.0).astype(jnp.bfloat16)
    right_mask = jnp.where(spot_lane >= LANES // 2, 0.0, 1.0).astype(jnp.bfloat16)
    spot = lax.broadcasted_iota(jnp.int32, kc_ref.shape, 1) - lax.broadcasted_iota(jnp.int32, kc_ref.shape, 0)
    cell_row = lax.broadcasted_iota(jnp.int32, kc_ref.shape, 0) // cc
    same = lax.broadcasted_iota(jnp.int32, kc_ref.shape, 1) // cc == cell_row
    kc_ref[...] = jnp.where(same, back_weight(spot.astype(jnp.float32), fog_sigma) * (1.0 / (POOL * POOL)), 0.0)
    lane = lax.broadcasted_iota(jnp.int32, (n, LANES), 1)
    sender = lax.broadcasted_iota(jnp.int32, (n, LANES), 0)
    source = (sender * cr + lane // cc).astype(jnp.float32)
    for i in range(cr):
        diff = source - (me * cr + i).astype(jnp.float32)
        wr[i] = jnp.where(lane < cr * cc, back_weight(diff, fog_sigma), 0.0)
    zero_side = jnp.zeros((rows + 2 * H, LANES), jnp.bfloat16)
    for x in (xh, xl):
        x[:, 0:LANES] = zero_side
        x[:, LANES + width :] = zero_side

    def coarse_message(step):
        total = jnp.zeros((1, LANES), jnp.float32)
        for a in range(cr):
            for j in range(cc):
                cell = jnp.sum(cs[a, :, j * POOL : (j + 1) * POOL], axis=1, keepdims=True)
                cell = jnp.sum(cell, axis=0, keepdims=True)
                total = total + cell * kc_ref[a * cc + j : a * cc + j + 1, :]
        msg[step] = total
        gath[step, me] = total

    def gather_start(step):
        def one(peer):
            pltpu.make_async_remote_copy(
                src_ref=msg.at[step], dst_ref=gath.at[step, me],
                send_sem=g_send.at[step], recv_sem=g_recv.at[step],
                device_id=peer, device_id_type=MESH,
            ).start()

        each_peer(one)

    def gather_copy(step):
        part = gath.at[step, pl.ds(0, n - 1)]
        return pltpu.make_async_remote_copy(
            src_ref=part, dst_ref=part, send_sem=g_send.at[step], recv_sem=g_recv.at[step],
            device_id=place(lax.rem(me + 1, n)), device_id_type=MESH,
        )

    def backscatter(step):
        gather_copy(step).wait_recv()
        whole = gath[step][:, 0, :]
        for i in range(cr):
            mixed = jnp.sum(wr[i] * whole, axis=0, keepdims=True)
            cells = mixed[:, 0:cc]
            for a in range(1, cr):
                cells = cells + mixed[:, a * cc : (a + 1) * cc]
            cells = ETA_BACK * cells
            for j in range(cc):
                backs[i, :, j * POOL : (j + 1) * POOL] = jnp.broadcast_to(cells[:, j : j + 1], (8, POOL))

    def halo(src_of, buf, send, recv, up):
        peer = me - 1 if up else me + 1
        slot = 1 if up else 0
        return pltpu.make_async_remote_copy(
            src_ref=src_of(0 if up else 1), dst_ref=buf.at[slot],
            send_sem=send.at[slot], recv_sem=recv.at[slot],
            device_id=place(lax.rem(peer + n, n)), device_id_type=MESH,
        )

    has_before, has_after = me > 0, me < n - 1

    def pat_edge(side):
        return pat_hbm.at[pl.ds(0 if side == 0 else rows - H, H)]

    def edge_of(side):
        return edge.at[side]

    def halo_start(src_of, buf, send, recv):
        @pl.when(has_before)
        def _():
            halo(src_of, buf, send, recv, True).start()

        @pl.when(has_after)
        def _():
            halo(src_of, buf, send, recv, False).start()

    def halo_recv(src_of, buf, send, recv, use):
        @pl.when(has_before)
        def _():
            halo(src_of, buf, send, recv, False).wait_recv()
            use(0)

        @pl.when(has_after)
        def _():
            halo(src_of, buf, send, recv, True).wait_recv()
            use(1)

    def halo_sent(src_of, buf, send, recv):
        @pl.when(has_before)
        def _():
            halo(src_of, buf, send, recv, True).wait_send()

        @pl.when(has_after)
        def _():
            halo(src_of, buf, send, recv, False).wait_send()

    def level(p):
        return jnp.where(p == 1, 5.0, jnp.where(p == 2, 7.0, 0.0)).astype(jnp.float32)

    own = pl.ds(LANES, width)
    for side in range(2):
        at = 0 if side == 0 else rows + H
        xh[pl.ds(at, H), own] = jnp.zeros((H, width), jnp.bfloat16)
        xl[pl.ds(at, H), own] = jnp.zeros((H, width), jnp.bfloat16)

    cs[...] = jnp.zeros_like(cs)
    for a in range(cr):
        loads[a].wait()

        @pl.loop(0, POOL // (2 * H))
        def _(k):
            row = pl.multiple_of(a * POOL + k * 2 * H, 2 * H)
            for j in range(cc):
                cols = pl.ds(j * POOL, POOL)
                value = level(pat[pl.ds(row, 2 * H), cols])
                xh[pl.ds(row + H, 2 * H), pl.ds(LANES + j * POOL, POOL)] = value.astype(jnp.bfloat16)
                cs[a, :, cols] += jnp.sum(value.reshape(2 * H // 8, 8, POOL), axis=0)

    cs[...] = cs[...] * 0.2
    coarse_message(0)
    pl.semaphore_wait(barrier, n - 1)
    gather_start(0)
    halo_start(pat_edge, hp, hp_send, hp_recv)

    def tile_cols(j, offset, count):
        return pl.ds(pl.multiple_of(j * POOL + offset, LANES), count)

    def window(ref, spans, cols):
        return jnp.concatenate([ref[pl.ds(at, count), cols] for at, count in spans], axis=0)

    def col_blur(first, j, spans):
        def rim(ref):
            count = sum(c for _, c in spans)
            left = window(ref, spans, tile_cols(j, 0, LANES))
            right = window(ref, spans, tile_cols(j, LANES + POOL, LANES))
            times = (count // H, 1)
            return left * jnp.tile(left_mask, times) + right * jnp.tile(right_mask, times)

        centre = tile_cols(j, LANES, POOL)
        high, rim_high = window(xh, spans, centre), rim(xh)
        if first:
            parts, table = [high, high, rim_high, rim_high], b1_ref
        else:
            parts, table = [high, high, window(xl, spans, centre), rim_high, rim(xl), rim_high], b2_ref
        value = jnp.dot(jnp.concatenate(parts, axis=1), table[...], preferred_element_type=jnp.float32)
        value_high, value_low = halves(value)
        done = 0
        for at, count in spans:
            yh[pl.ds(at, count), tile_cols(j, 0, POOL)] = value_high[done : done + count]
            yl[pl.ds(at, count), tile_cols(j, 0, POOL)] = value_low[done : done + count]
            done += count

    def row_blur(weights, j, row, count):
        cols = tile_cols(j, 0, POOL)
        high = yh[pl.ds(row, count + 2 * H), cols]
        low = yl[pl.ds(row, count + 2 * H), cols]
        return jnp.dot(weights[...], jnp.concatenate([high, high, low], axis=0), preferred_element_type=jnp.float32)

    def each_tile(fn, unroll):
        @pl.loop(0, cc // unroll)
        def _(k):
            for u in range(unroll):
                fn(k * unroll + u)

    def first_update(value, row, count, j):
        cols = tile_cols(j, 0, POOL)
        at = row
        while at < row + count:
            a = at // POOL
            part = min(row + count, (a + 1) * POOL) - at
            blk = pl.ds(at, part)
            p = pat[blk, cols]
            back = jnp.tile(backs[a, :, cols], (part // 8, 1))
            e = (value[at - row : at - row + part] + back) * (1.0 / (1.0 + ETA_BACK))
            dose = jnp.where(p > 0, jnp.where(p == 1, 1.5, 1.95) - e, 0.0)
            high, low = halves(dose)
            base[blk, cols] = jnp.where(p > 0, dose + jnp.where(p == 1, 0.5, 0.55), CLEAR)
            inside = tile_cols(j, LANES, POOL)
            xh[pl.ds(at + H, part), inside] = high
            xl[pl.ds(at + H, part), inside] = low
            cs[a, :, cols] += jnp.sum(dose.reshape(part // 8, 8, POOL), axis=0)
            if row == 0:
                edge[0, :, cols] = dose
            if row == rows - H:
                edge[1, :, cols] = dose
            at += part

    def last_store(value, row, count, j):
        fwd[pl.ds(row, count), tile_cols(j, 0, POOL)] = value

    def inner_rows(use):
        def one(j):
            for row in range(H, rows - H, TILE):
                use(row_blur(a_ref, j, row, TILE), row, TILE, j)

        each_tile(one, 4)

    def edge_rows(first, use):
        spans = ((0, H), (rows + H, H))
        each_tile(lambda j: col_blur(first, j, spans), 4)

        def one(j):
            for row in (0, rows - H):
                use(row_blur(e_ref, j, row, H), row, H, j)

        each_tile(one, 4)

    each_tile(lambda j: col_blur(True, j, ((H, rows),)), 4)
    cs[...] = jnp.zeros_like(cs)
    backscatter(0)
    inner_rows(first_update)

    def use_pattern(slot):
        at = 0 if slot == 0 else rows + H
        xh[pl.ds(at, H), own] = level(hp[slot]).astype(jnp.bfloat16)

    halo_recv(pat_edge, hp, hp_send, hp_recv, use_pattern)
    edge_rows(True, first_update)
    halo_start(edge_of, hd, hd_send, hd_recv)
    coarse_message(1)
    gather_start(1)
    each_tile(lambda j: col_blur(False, j, ((H, rows),)), 4)
    inner_rows(last_store)
    backscatter(1)

    def use_dose(slot):
        at = 0 if slot == 0 else rows + H
        high, low = halves(hd[slot])
        xh[pl.ds(at, H), own] = high
        xl[pl.ds(at, H), own] = low

    halo_recv(edge_of, hd, hd_send, hd_recv, use_dose)
    edge_rows(False, last_store)
    halo_sent(pat_edge, hp, hp_send, hp_recv)
    halo_sent(edge_of, hd, hd_send, hd_recv)
    for step in range(2):
        gather_copy(step).wait_send()


def finish_kernel(fwd, base, backs, dose_hbm, expo_hbm, dose, expo, sem):
    rows = fwd.shape[0]
    steps = rows // CHUNK

    def copies(k):
        blk = pl.ds(pl.multiple_of(k * CHUNK, CHUNK), CHUNK)
        return [
            pltpu.make_async_copy(src.at[blk], dst.at[blk], sem.at[i, k])
            for i, (src, dst) in enumerate(((dose, dose_hbm), (expo, expo_hbm)))
        ]

    for a in range(rows // POOL):

        @pl.loop(0, POOL // CHUNK)
        def _(k):
            step = a * (POOL // CHUNK) + k
            for r in range(0, CHUNK, 8):
                blk = pl.ds(pl.multiple_of(step * CHUNK + r, 8), 8)
                e = (fwd[blk, :] + backs[a]) * (1.0 / (1.0 + ETA_BACK))
                u = base[blk, :]
                expo[blk, :] = e
                dose[blk, :] = jnp.where(u == CLEAR, 0.0, u - e)
            for copy in copies(step):
                copy.start()

    @pl.loop(0, steps)
    def _(k):
        for copy in copies(k):
            copy.wait()


def solution(mesh):
    axes = tuple(mesh.axis_names)
    strips = mesh.shape["strip"]
    n = strips * mesh.shape["band"]

    def local(pattern):
        rows, width = pattern.shape
        cr, cc = rows // POOL, width // POOL

        vmem = pl.BlockSpec(memory_space=pltpu.VMEM)
        f32, bf16 = jnp.float32, jnp.bfloat16
        whole = jax.ShapeDtypeStruct((rows, width), f32)
        hbm = pl.BlockSpec(memory_space=pltpu.HBM)
        fwd, base, backs = pl.pallas_call(
            functools.partial(kernel, axes, n, strips),
            out_shape=(whole, whole, jax.ShapeDtypeStruct((cr, 8, width), f32)),
            in_specs=[hbm],
            out_specs=(vmem, vmem, vmem),
            scratch_shapes=[
                pltpu.VMEM((TILE, 3 * (TILE + 2 * H)), bf16),
                pltpu.VMEM((H, 3 * 3 * H), bf16),
                pltpu.VMEM((2 * (POOL + LANES), POOL), bf16),
                pltpu.VMEM((3 * (POOL + LANES), POOL), bf16),
                pltpu.VMEM((cr * cc, LANES), f32),
                pltpu.VMEM((rows, width), jnp.int32),
                pltpu.VMEM((2, H, width), jnp.int32),
                pltpu.VMEM((2, H, width), f32),
                pltpu.VMEM((2, H, width), f32),
                pltpu.VMEM((rows + 2 * H, width + 2 * LANES), bf16),
                pltpu.VMEM((rows + 2 * H, width + 2 * LANES), bf16),
                pltpu.VMEM((rows + 2 * H, width), bf16),
                pltpu.VMEM((rows + 2 * H, width), bf16),
                pltpu.VMEM((cr, 8, width), f32),
                pltpu.VMEM((2, 1, LANES), f32),
                pltpu.VMEM((2, n, 1, LANES), f32),
                pltpu.VMEM((cr, n, LANES), f32),
                pltpu.SemaphoreType.DMA((cr,)),
                pltpu.SemaphoreType.DMA((2,)),
                pltpu.SemaphoreType.DMA((2,)),
                pltpu.SemaphoreType.DMA((2,)),
                pltpu.SemaphoreType.DMA((2,)),
                pltpu.SemaphoreType.DMA((2,)),
                pltpu.SemaphoreType.DMA((2,)),
            ],
            compiler_params=pltpu.CompilerParams(
                collective_id=0, has_side_effects=True, vmem_limit_bytes=44 * 1024 * 1024
            ),
            name="proximity",
        )(pattern)
        return pl.pallas_call(
            finish_kernel,
            out_shape=(whole, whole),
            in_specs=[vmem] * 3,
            out_specs=(hbm, hbm),
            scratch_shapes=[
                pltpu.VMEM((rows, width), f32),
                pltpu.VMEM((rows, width), f32),
                pltpu.SemaphoreType.DMA((2, rows // CHUNK)),
            ],
            compiler_params=pltpu.CompilerParams(vmem_limit_bytes=20 * 1024 * 1024),
            name="finish",
        )(fwd, base, backs)

    return jax.shard_map(
        local,
        mesh=mesh,
        in_specs=(P(("band", "strip"), None),),
        out_specs=(P(("band", "strip"), None), P(("band", "strip"), None)),
        check_vma=False,
    )
```
